32 devices in a mesh: row: 16 (over z, x, core), col: 2 (over y).
Axes of the slice: x: 2, y: 2, z: 4, core: 2. Of those that a mesh axis runs over, the one named last changes fastest.
Arguments:
- counts: int32 [8192, 32768], P('row', 'col'), may hold values from 0 to 63
- row_support: int32 [8192], P(('row', 'col')), may hold values from 1 to 2209
- col_support: int32 [32768], P(('col', 'row')), may hold values from 1 to 2209
- total: int32 [1], replicated, may hold values from 256 to 4095
- sketch: bfloat16 [32768, 256], P('col'), may hold values from -6 to 6
Outputs:
- left_basis: float32 [8192, 256], P('row')
- right_basis: float32 [32768, 256], P('col')
The draws below stay inside these ranges and needn't reach their ends.
All inputs are finite; a program needn't handle non-finite values.
Results may differ from the reference program's by a relative error of at most 0.012.
Values may be sent and summed in bfloat16 or wider, within the bound.
A program may use at most 192 MiB of HBM per device.

```python
import jax
import jax.numpy as jnp
from jax import lax

N = 32768
K = 256
RB_DEV = 512
ROWS = 8192
N_ROW = 16


def support_values(key, length):
    first = jax.random.randint(jax.random.fold_in(key, 11), (length,), 1, 48)
    second = jax.random.randint(jax.random.fold_in(key, 23), (length,), 1, 48)
    return (first * second).astype(jnp.int32)


def draw_row_support(key, part):
    return support_values(jax.random.fold_in(key, 5), ROWS)


def draw_col_support(key, part):
    return support_values(jax.random.fold_in(key, 7), N)


def touch_ends(values, own_key, smallest, high):
    extent = values.shape
    index_at = [jax.random.randint(jax.random.fold_in(own_key, axis), (), 0, extent[axis]) for axis in range(len(extent))]
    values = values.at[tuple(index_at)].set(smallest)
    longest = extent.index(max(extent))
    index_at[longest] = (index_at[longest] + 1) % extent[longest]
    return values.at[tuple(index_at)].set(high)


def block_scale(own_key, extent, shards, low, top_value):
    def one(dim, blocks):
        draws = jax.random.uniform(jax.random.fold_in(jax.random.fold_in(own_key, 6), dim), (blocks,), jnp.float32, low / len(shards), top_value / len(shards))
        return jnp.repeat(jnp.exp(draws), extent[dim] // blocks).reshape((-1,) + (1,) * (len(extent) - dim - 1))

    loudness = one(*shards[0])
    for cut in shards[1:]:
        loudness = loudness * one(*cut)
    return loudness


def centred(own_key, dims, spread, most, shards=(), kind=jnp.bfloat16):
    values = spread * jax.random.normal(own_key, dims, jnp.float32)
    if shards:
        values = values * block_scale(own_key, dims, shards, -0.22, 0.18)
    return jnp.clip(values, -most, most).astype(kind)


def setup_inputs(seed: int = 0) -> dict:
    splits = jax.random.split(jax.random.key(seed), 6)
    return {
        "counts": touch_ends(jax.random.randint(splits[0], (ROWS, N), 0, 64), jax.random.fold_in(splits[0], 1), 0, 63).astype(jnp.int32),
        "row_support": draw_row_support(jax.random.fold_in(splits[5], 71), 0),
        "col_support": draw_col_support(jax.random.fold_in(splits[5], 71), 0),
        "total": jax.random.randint(splits[3], (1,), 256, 4096).astype(jnp.int32),
        "sketch": centred(splits[4], (N, K), 1.0, 6.0, ((0, 2),)),
    }


def lift(block, row_part, col_support, total):
    value = jnp.log(jnp.maximum(block, 1).astype(jnp.float32))
    value = value + jnp.log(total[0].astype(jnp.float32))
    value = value - jnp.log(row_part.astype(jnp.float32))[:, None]
    value = value - jnp.log(col_support.astype(jnp.float32))[None, :]
    return jnp.where(block > 0, jnp.maximum(value, 0.0), 0.0).astype(jnp.bfloat16)

def orthonormal(matrix):
    gram = jnp.dot(matrix.T, matrix, precision=lax.Precision.HIGHEST)
    lower = jnp.linalg.cholesky(gram)
    return jax.scipy.linalg.solve_triangular(lower, matrix.T, lower=True).T

def reference(counts, row_support, col_support, total, sketch):
    blocks = counts.reshape(N_ROW, RB_DEV, N)
    supports = row_support.reshape(N_ROW, RB_DEV)

    def apply_right(rhs):

        def one(pair):
            table = lift(pair[0], pair[1], col_support, total)
            return jnp.dot(table.astype(jnp.float32), rhs.astype(jnp.float32), preferred_element_type=jnp.float32)
        return lax.map(one, (blocks, supports)).reshape(ROWS, K)

    def apply_left(lhs):
        lhs_blocks = lhs.reshape(N_ROW, RB_DEV, K)

        def step(carry, trio):
            table = lift(trio[0], trio[1], col_support, total)
            part = lax.dot_general(table.astype(jnp.float32), trio[2].astype(jnp.float32), (((0,), (0,)), ((), ())), preferred_element_type=jnp.float32)
            return (carry + part, None)
        start = jnp.zeros((N, K), jnp.float32)
        result, _ = lax.scan(step, start, (blocks, supports, lhs_blocks))
        return result
    q_first = orthonormal(apply_right(sketch)).astype(jnp.bfloat16)
    q_second = orthonormal(apply_left(q_first))
    q_third = orthonormal(apply_right(q_second.astype(jnp.bfloat16)))
    return (q_third * jnp.sqrt(jnp.float32(ROWS)), q_second * jnp.sqrt(jnp.float32(N)))
```

```python
import jax
import jax.numpy as jnp
from jax import lax
from jax.experimental import pallas as pl
from jax.experimental.pallas import tpu as pltpu
from jax.sharding import PartitionSpec as P

HIGHEST = lax.Precision.HIGHEST
BLOCK = 32


def lift(block, row_part, col_part, total):
    value = jnp.log(jnp.maximum(block, 1).astype(jnp.float32))
    value = value + jnp.log(total[0].astype(jnp.float32))
    value = value - jnp.log(row_part.astype(jnp.float32))[:, None]
    value = value - jnp.log(col_part.astype(jnp.float32))[None, :]
    return jnp.where(block > 0, jnp.maximum(value, 0.0), 0.0).astype(jnp.bfloat16)


def factor_step(rest, inverse, lower_ref, base):
    size = rest.shape[0]
    lanes = 128
    corner = rest[:BLOCK, :lanes]
    row = lax.broadcasted_iota(jnp.int32, (BLOCK, lanes), 0)
    lane = lax.broadcasted_iota(jnp.int32, (BLOCK, lanes), 1)
    unit = jnp.where(lane - BLOCK == row, 1.0, 0.0)
    work = jnp.where(lane < BLOCK, corner, unit)
    pivots = jnp.ones((BLOCK, 1), jnp.float32)
    for j in range(BLOCK):
        pivot = work[j : j + 1, j : j + 1]
        scaled = work[j : j + 1, :] * (1.0 / pivot)
        column = jnp.where(row > j, work[:, j : j + 1], 0.0)
        work = work - column * scaled
        pivots = jnp.where(row[:, :1] == j, pivot, pivots)
    work = work * lax.rsqrt(pivots)
    small = pltpu.roll(work, lanes - BLOCK, 1)[:, :BLOCK]
    panel = jnp.dot(small, rest[:BLOCK, :], precision=HIGHEST, preferred_element_type=jnp.float32)
    done = jnp.dot(small, inverse[:BLOCK, :], precision=HIGHEST, preferred_element_type=jnp.float32)
    lower_ref[pl.ds(pl.multiple_of(base, BLOCK), BLOCK), :] = done
    panel = pltpu.roll(panel, size - BLOCK, 1)
    down = (((0,), (0,)), ((), ()))
    rest_cut = lax.dot_general(panel, panel, down, precision=HIGHEST, preferred_element_type=jnp.float32)
    inverse_cut = lax.dot_general(panel, done, down, precision=HIGHEST, preferred_element_type=jnp.float32)
    return rest_cut, inverse_cut


def invert_factor(gram_ref, lower_ref, rest_ref, inverse_ref):
    size = gram_ref.shape[0]
    rest_ref[:size, :] = gram_ref[...]
    rest_ref[size:, :] = jnp.zeros((BLOCK, size), jnp.float32)
    row = lax.broadcasted_iota(jnp.int32, (size, size), 0)
    lane = lax.broadcasted_iota(jnp.int32, (size, size), 1)
    inverse_ref[:size, :] = jnp.where(row == lane, 1.0, 0.0)
    inverse_ref[size:, :] = jnp.zeros((BLOCK, size), jnp.float32)

    def body(step, carry):
        rest_cut, inverse_cut = factor_step(rest_ref[:size, :], inverse_ref[:size, :], lower_ref, step * BLOCK)
        rest_ref[:size, :] = pltpu.roll(rest_ref[BLOCK:, :], size - BLOCK, 1) - rest_cut
        inverse_ref[:size, :] = inverse_ref[BLOCK:, :] - inverse_cut
        return carry

    lax.fori_loop(0, size // BLOCK, body, 0)


def inverse_factor(gram):
    size = gram.shape[0]
    return pl.pallas_call(
        invert_factor,
        out_shape=jax.ShapeDtypeStruct((size, size), jnp.float32),
        in_specs=[pl.BlockSpec(memory_space=pltpu.VMEM)],
        out_specs=pl.BlockSpec(memory_space=pltpu.VMEM),
        scratch_shapes=[
            pltpu.VMEM((size + BLOCK, size), jnp.float32),
            pltpu.VMEM((size + BLOCK, size), jnp.float32),
        ],
    )(gram)


def sum_scatter(value, axis):
    count = lax.axis_size(axis)
    if count != 2:
        return lax.psum_scatter(value, axis, scatter_dimension=0, tiled=True)
    here = lax.axis_index(axis)
    rows = value.shape[0] // 2
    sent = lax.dynamic_slice_in_dim(value, (1 - here) * rows, rows, 0)
    got = lax.ppermute(sent, axis, [(0, 1), (1, 0)])
    return lax.dynamic_slice_in_dim(value, here * rows, rows, 0) + got


def gather(value, axis):
    count = lax.axis_size(axis)
    if count != 2:
        return lax.all_gather(value, axis, axis=0, tiled=True)
    other = lax.ppermute(value, axis, [(0, 1), (1, 0)])
    first = lax.axis_index(axis) == 0
    return jnp.concatenate([jnp.where(first, value, other), jnp.where(first, other, value)], 0)


def orth(part):
    gram = lax.dot_general(part, part, (((0,), (0,)), ((), ())), precision=HIGHEST)
    gram = lax.psum(gram, ("row", "col"))
    lower = inverse_factor(gram)
    return lax.dot_general(part, lower, (((1,), (1,)), ((), ())), precision=HIGHEST)


def per_device(counts, row_support, col_support, total, sketch):
    row_local = lax.all_gather(row_support, "col", axis=0, tiled=True)
    col_local = lax.all_gather(col_support, "row", axis=0, tiled=True)
    table = lift(counts, row_local, col_local, total)
    total_rows = table.shape[0] * lax.axis_size("row")
    total_cols = table.shape[1] * lax.axis_size("col")

    first = sum_scatter(jnp.dot(table, sketch, preferred_element_type=jnp.float32), "col")
    q_first = gather(orth(first).astype(jnp.bfloat16), "col")
    partial_value = lax.dot_general(
        table, q_first, (((0,), (0,)), ((), ())), preferred_element_type=jnp.float32
    )
    second = lax.psum_scatter(partial_value, "row", scatter_dimension=0, tiled=True)
    q_second = lax.all_gather(orth(second).astype(jnp.bfloat16), "row", axis=0, tiled=True)
    third = sum_scatter(jnp.dot(table, q_second, preferred_element_type=jnp.float32), "col")
    q_third = gather(orth(third) * jnp.sqrt(jnp.float32(total_rows)), "col")
    return q_third, q_second.astype(jnp.float32) * jnp.sqrt(jnp.float32(total_cols))


def solution(mesh):
    in_specs = (P("row", "col"), P(("row", "col")), P(("col", "row")), P(), P("col", None))
    out_specs = (P("row", None), P("col", None))
    return jax.shard_map(
        per_device, mesh=mesh, in_specs=in_specs, out_specs=out_specs, check_vma=False
    )
```

```python
import functools

import jax
import jax.numpy as jnp
from jax import lax
from jax.experimental import pallas as pl
from jax.experimental.pallas import tpu as pltpu
from jax.sharding import PartitionSpec as P

HIGHEST = lax.Precision.HIGHEST
MESH = pl.DeviceIdType.MESH
BLOCK = 32


def lift(block, row_part, col_part, total):
    value = jnp.log(jnp.maximum(block, 1).astype(jnp.float32))
    value = value + jnp.log(total[0].astype(jnp.float32))
    value = value - jnp.log(row_part.astype(jnp.float32))[:, None]
    value = value - jnp.log(col_part.astype(jnp.float32))[None, :]
    return jnp.where(block > 0, jnp.maximum(value, 0.0), 0.0).astype(jnp.bfloat16)


def factor_step(rest, inverse, lower_ref, base):
    size = rest.shape[0]
    lanes = 128
    corner = rest[:BLOCK, :lanes]
    row = lax.broadcasted_iota(jnp.int32, (BLOCK, lanes), 0)
    lane = lax.broadcasted_iota(jnp.int32, (BLOCK, lanes), 1)
    unit = jnp.where(lane - BLOCK == row, 1.0, 0.0)
    work = jnp.where(lane < BLOCK, corner, unit)
    pivots = jnp.ones((BLOCK, 1), jnp.float32)
    for j in range(BLOCK):
        pivot = work[j : j + 1, j : j + 1]
        scaled = work[j : j + 1, :] * (1.0 / pivot)
        column = jnp.where(row > j, work[:, j : j + 1], 0.0)
        work = work - column * scaled
        pivots = jnp.where(row[:, :1] == j, pivot, pivots)
    work = work * lax.rsqrt(pivots)
    small = pltpu.roll(work, lanes - BLOCK, 1)[:, :BLOCK]
    panel = jnp.dot(small, rest[:BLOCK, :], precision=HIGHEST, preferred_element_type=jnp.float32)
    done = jnp.dot(small, inverse[:BLOCK, :], precision=HIGHEST, preferred_element_type=jnp.float32)
    lower_ref[pl.ds(pl.multiple_of(base, BLOCK), BLOCK), :] = done
    panel = pltpu.roll(panel, size - BLOCK, 1)
    down = (((0,), (0,)), ((), ()))
    rest_cut = lax.dot_general(panel, panel, down, precision=HIGHEST, preferred_element_type=jnp.float32)
    inverse_cut = lax.dot_general(panel, done, down, precision=HIGHEST, preferred_element_type=jnp.float32)
    return rest_cut, inverse_cut


def invert_factor(gram_ref, lower_ref, rest_ref, inverse_ref):
    size = gram_ref.shape[0]
    rest_ref[:size, :] = gram_ref[...]
    rest_ref[size:, :] = jnp.zeros((BLOCK, size), jnp.float32)
    row = lax.broadcasted_iota(jnp.int32, (size, size), 0)
    lane = lax.broadcasted_iota(jnp.int32, (size, size), 1)
    inverse_ref[:size, :] = jnp.where(row == lane, 1.0, 0.0)
    inverse_ref[size:, :] = jnp.zeros((BLOCK, size), jnp.float32)

    def body(step, carry):
        rest_cut, inverse_cut = factor_step(rest_ref[:size, :], inverse_ref[:size, :], lower_ref, step * BLOCK)
        rest_ref[:size, :] = pltpu.roll(rest_ref[BLOCK:, :], size - BLOCK, 1) - rest_cut
        inverse_ref[:size, :] = inverse_ref[BLOCK:, :] - inverse_cut
        return carry

    lax.fori_loop(0, size // BLOCK, body, 0)


def inverse_factor(gram):
    size = gram.shape[0]
    return pl.pallas_call(
        invert_factor,
        out_shape=jax.ShapeDtypeStruct((size, size), jnp.float32),
        in_specs=[pl.BlockSpec(memory_space=pltpu.VMEM)],
        out_specs=pl.BlockSpec(memory_space=pltpu.VMEM),
        scratch_shapes=[
            pltpu.VMEM((size + BLOCK, size), jnp.float32),
            pltpu.VMEM((size + BLOCK, size), jnp.float32),
        ],
    )(gram)


def place(index, cols):
    return (lax.div(index, cols), lax.rem(index, cols))


def greet(count, cols, me):
    barrier = pltpu.get_barrier_semaphore()

    def hello(step, carry):
        peer = lax.rem(me + step, count)
        pl.semaphore_signal(barrier, inc=1, device_id=place(peer, cols), device_id_type=MESH)
        return carry

    lax.fori_loop(1, count, hello, 0)
    pl.semaphore_wait(barrier, count - 1)


def reduce_kernel(count, cols, part_ref, total_ref, inbox, mine, send_a, recv_a, send_b, recv_b):
    me = lax.axis_index("row") * cols + lax.axis_index("col")
    rows = part_ref.shape[0] // count
    greet(count, cols, me)

    def rows_of(index):
        return pl.ds(pl.multiple_of(index * rows, rows), rows)

    def scatter_copy(step):
        peer = lax.rem(me + step, count)
        return pltpu.make_async_remote_copy(
            src_ref=part_ref.at[rows_of(peer), :],
            dst_ref=inbox.at[me],
            send_sem=send_a.at[step],
            recv_sem=recv_a.at[me],
            device_id=place(peer, cols),
            device_id_type=MESH,
        )

    def arrival(step):
        peer = lax.rem(me + count - step, count)
        return pltpu.make_async_remote_copy(
            src_ref=part_ref.at[rows_of(me), :],
            dst_ref=inbox.at[peer],
            send_sem=send_a.at[step],
            recv_sem=recv_a.at[peer],
            device_id=place(peer, cols),
            device_id_type=MESH,
        )

    def spread_copy(step):
        peer = lax.rem(me + step, count)
        return pltpu.make_async_remote_copy(
            src_ref=mine,
            dst_ref=total_ref.at[rows_of(me), :],
            send_sem=send_b.at[step],
            recv_sem=recv_b.at[me],
            device_id=place(peer, cols),
            device_id_type=MESH,
        )

    def spread_arrival(step):
        peer = lax.rem(me + count - step, count)
        return pltpu.make_async_remote_copy(
            src_ref=mine,
            dst_ref=total_ref.at[rows_of(peer), :],
            send_sem=send_b.at[step],
            recv_sem=recv_b.at[peer],
            device_id=place(peer, cols),
            device_id_type=MESH,
        )

    def each(action):
        def body(step, carry):
            action(step)
            return carry

        lax.fori_loop(1, count, body, 0)

    each(lambda step: scatter_copy(step).start())
    inbox[me] = part_ref[rows_of(me), :]
    each(lambda step: arrival(step).wait_recv())
    total = inbox[0]
    for index in range(1, count):
        total = total + inbox[index]
    mine[...] = total
    each(lambda step: spread_copy(step).start())
    total_ref[rows_of(me), :] = total
    each(lambda step: spread_arrival(step).wait_recv())
    each(lambda step: scatter_copy(step).wait_send())
    each(lambda step: spread_copy(step).wait_send())


def whole_sum(value):
    cols = lax.axis_size("col")
    count = lax.axis_size("row") * cols
    size, width = value.shape
    rows = size // count
    if size % (8 * count) or width % 128:
        return lax.psum(value, ("row", "col"))
    sems = pltpu.SemaphoreType.DMA((count,))
    return pl.pallas_call(
        functools.partial(reduce_kernel, count, cols),
        out_shape=jax.ShapeDtypeStruct(value.shape, value.dtype),
        in_specs=[pl.BlockSpec(memory_space=pltpu.VMEM)],
        out_specs=pl.BlockSpec(memory_space=pltpu.VMEM),
        scratch_shapes=[
            pltpu.VMEM((count, rows, width), value.dtype),
            pltpu.VMEM((rows, width), value.dtype),
            sems,
            sems,
            sems,
            sems,
        ],
        compiler_params=pltpu.CompilerParams(collective_id=0, has_side_effects=True),
    )(value)


def support_kernel(n_row, n_col, row_ref, col_ref, row_all, col_all, send_sem, recv_sem):
    row, col = lax.axis_index("row"), lax.axis_index("col")

    def across(step):
        return (row, lax.rem(col + step, n_col))

    def down(step):
        return (lax.rem(row + step, n_row), col)

    barrier = pltpu.get_barrier_semaphore()
    peers = [across(step) for step in range(1, n_col)] + [down(step) for step in range(1, n_row)]
    for peer in peers:
        pl.semaphore_signal(barrier, inc=1, device_id=peer, device_id_type=MESH)
    pl.semaphore_wait(barrier, len(peers))

    def copy(ref, into, slot, lane, peer):
        return pltpu.make_async_remote_copy(
            src_ref=ref,
            dst_ref=into.at[slot],
            send_sem=send_sem.at[lane],
            recv_sem=recv_sem.at[lane],
            device_id=peer,
            device_id_type=MESH,
        )

    sends, waits = [], []
    for step in range(1, n_col):
        lane = step - 1
        sends.append(copy(row_ref, row_all, col, lane, across(step)))
        waits.append(copy(row_ref, row_all, lax.rem(col + n_col - step, n_col), lane, across(step)))
    for step in range(1, n_row):
        lane = n_col - 1 + step - 1
        sends.append(copy(col_ref, col_all, row, lane, down(step)))
        waits.append(copy(col_ref, col_all, lax.rem(row + n_row - step, n_row), lane, down(step)))
    for item in sends:
        item.start()
    row_all[col] = row_ref[...]
    col_all[row] = col_ref[...]
    for item in waits:
        item.wait_recv()
    for item in sends:
        item.wait_send()


def gather_supports(row_support, col_support):
    n_row, n_col = lax.axis_size("row"), lax.axis_size("col")
    row_len, col_len = row_support.shape[0], col_support.shape[0]
    if row_len % 128 or col_len % 128:
        row_local = lax.all_gather(row_support, "col", axis=0, tiled=True)
        return row_local, lax.all_gather(col_support, "row", axis=0, tiled=True)
    lanes = n_row + n_col - 2
    vmem = pl.BlockSpec(memory_space=pltpu.VMEM)
    row_all, col_all = pl.pallas_call(
        functools.partial(support_kernel, n_row, n_col),
        out_shape=[
            jax.ShapeDtypeStruct((n_col, row_len // 128, 128), row_support.dtype),
            jax.ShapeDtypeStruct((n_row, col_len // 128, 128), col_support.dtype),
        ],
        in_specs=[vmem, vmem],
        out_specs=[vmem, vmem],
        scratch_shapes=[pltpu.SemaphoreType.DMA((lanes,)), pltpu.SemaphoreType.DMA((lanes,))],
        compiler_params=pltpu.CompilerParams(collective_id=1, has_side_effects=True),
    )(row_support.reshape(-1, 128), col_support.reshape(-1, 128))
    return row_all.reshape(-1), col_all.reshape(-1)


def sum_scatter(value, axis):
    count = lax.axis_size(axis)
    if count != 2:
        return lax.psum_scatter(value, axis, scatter_dimension=0, tiled=True)
    here = lax.axis_index(axis)
    rows = value.shape[0] // 2
    sent = lax.dynamic_slice_in_dim(value, (1 - here) * rows, rows, 0)
    got = lax.ppermute(sent, axis, [(0, 1), (1, 0)])
    return lax.dynamic_slice_in_dim(value, here * rows, rows, 0) + got


def gather(value, axis):
    count = lax.axis_size(axis)
    if count != 2:
        return lax.all_gather(value, axis, axis=0, tiled=True)
    other = lax.ppermute(value, axis, [(0, 1), (1, 0)])
    first = lax.axis_index(axis) == 0
    return jnp.concatenate([jnp.where(first, value, other), jnp.where(first, other, value)], 0)


def orth(part):
    gram = lax.dot_general(part, part, (((0,), (0,)), ((), ())), precision=HIGHEST)
    lower = inverse_factor(whole_sum(gram))
    return lax.dot_general(part, lower, (((1,), (1,)), ((), ())), precision=HIGHEST)


def per_device(counts, row_support, col_support, total, sketch):
    row_local, col_local = gather_supports(row_support, col_support)
    table = lift(counts, row_local, col_local, total)
    total_rows = table.shape[0] * lax.axis_size("row")
    total_cols = table.shape[1] * lax.axis_size("col")

    first = sum_scatter(jnp.dot(table, sketch, preferred_element_type=jnp.float32), "col")
    q_first = gather(orth(first).astype(jnp.bfloat16), "col")
    partial_value = lax.dot_general(
        table, q_first, (((0,), (0,)), ((), ())), preferred_element_type=jnp.float32
    )
    second = lax.psum_scatter(partial_value, "row", scatter_dimension=0, tiled=True)
    q_second = lax.all_gather(orth(second).astype(jnp.bfloat16), "row", axis=0, tiled=True)
    third = sum_scatter(jnp.dot(table, q_second, preferred_element_type=jnp.float32), "col")
    q_third = gather(orth(third) * jnp.sqrt(jnp.float32(total_rows)), "col")
    return q_third, q_second.astype(jnp.float32) * jnp.sqrt(jnp.float32(total_cols))


def solution(mesh):
    in_specs = (P("row", "col"), P(("row", "col")), P(("col", "row")), P(), P("col", None))
    out_specs = (P("row", None), P("col", None))
    return jax.shard_map(
        per_device, mesh=mesh, in_specs=in_specs, out_specs=out_specs, check_vma=False
    )
```

```python
import functools
import math

import jax
import jax.numpy as jnp
from jax import lax
from jax.experimental import pallas as pl
from jax.experimental.pallas import tpu as pltpu
from jax.sharding import PartitionSpec as P

HIGHEST = lax.Precision.HIGHEST
MESH = pl.DeviceIdType.MESH
BLOCK = 32


def lift(block, row_part, col_part, total):
    value = jnp.log(jnp.maximum(block, 1).astype(jnp.float32))
    value = value + jnp.log(total[0].astype(jnp.float32))
    value = value - jnp.log(row_part.astype(jnp.float32))[:, None]
    value = value - jnp.log(col_part.astype(jnp.float32))[None, :]
    return jnp.where(block > 0, jnp.maximum(value, 0.0), 0.0).astype(jnp.bfloat16)


def factor_step(rest, inverse, lower_ref, base):
    size = rest.shape[0]
    lanes = 128
    corner = rest[:BLOCK, :lanes]
    row = lax.broadcasted_iota(jnp.int32, (BLOCK, lanes), 0)
    lane = lax.broadcasted_iota(jnp.int32, (BLOCK, lanes), 1)
    unit = jnp.where(lane - BLOCK == row, 1.0, 0.0)
    work = jnp.where(lane < BLOCK, corner, unit)
    pivots = jnp.ones((BLOCK, 1), jnp.float32)
    for j in range(BLOCK):
        pivot = work[j : j + 1, j : j + 1]
        scaled = work[j : j + 1, :] * (1.0 / pivot)
        column = jnp.where(row > j, work[:, j : j + 1], 0.0)
        work = work - column * scaled
        pivots = jnp.where(row[:, :1] == j, pivot, pivots)
    work = work * lax.rsqrt(pivots)
    small = pltpu.roll(work, lanes - BLOCK, 1)[:, :BLOCK]
    panel = jnp.dot(small, rest[:BLOCK, :], precision=HIGHEST, preferred_element_type=jnp.float32)
    done = jnp.dot(small, inverse[:BLOCK, :], precision=HIGHEST, preferred_element_type=jnp.float32)
    lower_ref[pl.ds(pl.multiple_of(base, BLOCK), BLOCK), :] = done
    panel = pltpu.roll(panel, size - BLOCK, 1)
    down = (((0,), (0,)), ((), ()))
    rest_cut = lax.dot_general(panel, panel, down, precision=HIGHEST, preferred_element_type=jnp.float32)
    inverse_cut = lax.dot_general(panel, done, down, precision=HIGHEST, preferred_element_type=jnp.float32)
    return rest_cut, inverse_cut


def invert_factor(gram_ref, lower_ref, rest_ref, inverse_ref):
    size = gram_ref.shape[0]
    rest_ref[:size, :] = gram_ref[...]
    rest_ref[size:, :] = jnp.zeros((BLOCK, size), jnp.float32)
    row = lax.broadcasted_iota(jnp.int32, (size, size), 0)
    lane = lax.broadcasted_iota(jnp.int32, (size, size), 1)
    inverse_ref[:size, :] = jnp.where(row == lane, 1.0, 0.0)
    inverse_ref[size:, :] = jnp.zeros((BLOCK, size), jnp.float32)

    def body(step, carry):
        rest_cut, inverse_cut = factor_step(rest_ref[:size, :], inverse_ref[:size, :], lower_ref, step * BLOCK)
        rest_ref[:size, :] = pltpu.roll(rest_ref[BLOCK:, :], size - BLOCK, 1) - rest_cut
        inverse_ref[:size, :] = inverse_ref[BLOCK:, :] - inverse_cut
        return carry

    lax.fori_loop(0, size // BLOCK, body, 0)


def inverse_factor(gram):
    size = gram.shape[0]
    return pl.pallas_call(
        invert_factor,
        out_shape=jax.ShapeDtypeStruct((size, size), jnp.float32),
        in_specs=[pl.BlockSpec(memory_space=pltpu.VMEM)],
        out_specs=pl.BlockSpec(memory_space=pltpu.VMEM),
        scratch_shapes=[
            pltpu.VMEM((size + BLOCK, size), jnp.float32),
            pltpu.VMEM((size + BLOCK, size), jnp.float32),
        ],
    )(gram)


def place(index, cols):
    return (lax.div(index, cols), lax.rem(index, cols))


def greet(count, cols, me):
    barrier = pltpu.get_barrier_semaphore()

    def hello(step, carry):
        peer = lax.rem(me + step, count)
        pl.semaphore_signal(barrier, inc=1, device_id=place(peer, cols), device_id_type=MESH)
        return carry

    lax.fori_loop(1, count, hello, 0)
    pl.semaphore_wait(barrier, count - 1)


def reduce_kernel(count, cols, part_ref, total_ref, inbox, mine, send_a, recv_a, send_b, recv_b):
    me = lax.axis_index("row") * cols + lax.axis_index("col")
    rows = part_ref.shape[0] // count
    greet(count, cols, me)

    def rows_of(index):
        return pl.ds(pl.multiple_of(index * rows, rows), rows)

    def scatter_copy(step):
        peer = lax.rem(me + step, count)
        return pltpu.make_async_remote_copy(
            src_ref=part_ref.at[rows_of(peer), :],
            dst_ref=inbox.at[me],
            send_sem=send_a.at[step],
            recv_sem=recv_a.at[me],
            device_id=place(peer, cols),
            device_id_type=MESH,
        )

    def arrival(step):
        peer = lax.rem(me + count - step, count)
        return pltpu.make_async_remote_copy(
            src_ref=part_ref.at[rows_of(me), :],
            dst_ref=inbox.at[peer],
            send_sem=send_a.at[step],
            recv_sem=recv_a.at[peer],
            device_id=place(peer, cols),
            device_id_type=MESH,
        )

    def spread_copy(step):
        peer = lax.rem(me + step, count)
        return pltpu.make_async_remote_copy(
            src_ref=mine,
            dst_ref=total_ref.at[rows_of(me), :],
            send_sem=send_b.at[step],
            recv_sem=recv_b.at[me],
            device_id=place(peer, cols),
            device_id_type=MESH,
        )

    def spread_arrival(step):
        peer = lax.rem(me + count - step, count)
        return pltpu.make_async_remote_copy(
            src_ref=mine,
            dst_ref=total_ref.at[rows_of(peer), :],
            send_sem=send_b.at[step],
            recv_sem=recv_b.at[peer],
            device_id=place(peer, cols),
            device_id_type=MESH,
        )

    def each(action):
        def body(step, carry):
            action(step)
            return carry

        lax.fori_loop(1, count, body, 0)

    each(lambda step: scatter_copy(step).start())
    inbox[me] = part_ref[rows_of(me), :]
    each(lambda step: arrival(step).wait_recv())
    total = inbox[0]
    for index in range(1, count):
        total = total + inbox[index]
    mine[...] = total
    each(lambda step: spread_copy(step).start())
    total_ref[rows_of(me), :] = total
    each(lambda step: spread_arrival(step).wait_recv())
    each(lambda step: scatter_copy(step).wait_send())
    each(lambda step: spread_copy(step).wait_send())


def whole_sum(value):
    cols = lax.axis_size("col")
    count = lax.axis_size("row") * cols
    size, width = value.shape
    rows = size // count
    if size % (8 * count) or width % 128:
        return lax.psum(value, ("row", "col"))
    sems = pltpu.SemaphoreType.DMA((count,))
    return pl.pallas_call(
        functools.partial(reduce_kernel, count, cols),
        out_shape=jax.ShapeDtypeStruct(value.shape, value.dtype),
        in_specs=[pl.BlockSpec(memory_space=pltpu.VMEM)],
        out_specs=pl.BlockSpec(memory_space=pltpu.VMEM),
        scratch_shapes=[
            pltpu.VMEM((count, rows, width), value.dtype),
            pltpu.VMEM((rows, width), value.dtype),
            sems,
            sems,
            sems,
            sems,
        ],
        compiler_params=pltpu.CompilerParams(collective_id=0, has_side_effects=True),
    )(value)


def support_kernel(n_row, n_col, row_ref, col_ref, row_all, col_all, send_sem, recv_sem):
    row, col = lax.axis_index("row"), lax.axis_index("col")

    def across(step):
        return (row, lax.rem(col + step, n_col))

    def down(step):
        return (lax.rem(row + step, n_row), col)

    barrier = pltpu.get_barrier_semaphore()
    peers = [across(step) for step in range(1, n_col)] + [down(step) for step in range(1, n_row)]
    for peer in peers:
        pl.semaphore_signal(barrier, inc=1, device_id=peer, device_id_type=MESH)
    pl.semaphore_wait(barrier, len(peers))

    def copy(ref, into, slot, lane, peer):
        return pltpu.make_async_remote_copy(
            src_ref=ref,
            dst_ref=into.at[slot],
            send_sem=send_sem.at[lane],
            recv_sem=recv_sem.at[lane],
            device_id=peer,
            device_id_type=MESH,
        )

    sends, waits = [], []
    for step in range(1, n_col):
        lane = step - 1
        sends.append(copy(row_ref, row_all, col, lane, across(step)))
        waits.append(copy(row_ref, row_all, lax.rem(col + n_col - step, n_col), lane, across(step)))
    for step in range(1, n_row):
        lane = n_col - 1 + step - 1
        sends.append(copy(col_ref, col_all, row, lane, down(step)))
        waits.append(copy(col_ref, col_all, lax.rem(row + n_row - step, n_row), lane, down(step)))
    for item in sends:
        item.start()
    row_all[col] = row_ref[...]
    col_all[row] = col_ref[...]
    for item in waits:
        item.wait_recv()
    for item in sends:
        item.wait_send()


def gather_supports(row_support, col_support):
    n_row, n_col = lax.axis_size("row"), lax.axis_size("col")
    row_len, col_len = row_support.shape[0], col_support.shape[0]
    if row_len % 128 or col_len % 128:
        row_local = lax.all_gather(row_support, "col", axis=0, tiled=True)
        return row_local, lax.all_gather(col_support, "row", axis=0, tiled=True)
    lanes = n_row + n_col - 2
    vmem = pl.BlockSpec(memory_space=pltpu.VMEM)
    row_all, col_all = pl.pallas_call(
        functools.partial(support_kernel, n_row, n_col),
        out_shape=[
            jax.ShapeDtypeStruct((n_col, row_len // 128, 128), row_support.dtype),
            jax.ShapeDtypeStruct((n_row, col_len // 128, 128), col_support.dtype),
        ],
        in_specs=[vmem, vmem],
        out_specs=[vmem, vmem],
        scratch_shapes=[pltpu.SemaphoreType.DMA((lanes,)), pltpu.SemaphoreType.DMA((lanes,))],
        compiler_params=pltpu.CompilerParams(collective_id=1, has_side_effects=True),
    )(row_support.reshape(-1, 128), col_support.reshape(-1, 128))
    return row_all.reshape(-1), col_all.reshape(-1)


def sum_scatter(value, axis):
    count = lax.axis_size(axis)
    if count != 2:
        return lax.psum_scatter(value, axis, scatter_dimension=0, tiled=True)
    here = lax.axis_index(axis)
    rows = value.shape[0] // 2
    sent = lax.dynamic_slice_in_dim(value, (1 - here) * rows, rows, 0)
    got = lax.ppermute(sent, axis, [(0, 1), (1, 0)])
    return lax.dynamic_slice_in_dim(value, here * rows, rows, 0) + got


def gather(value, axis):
    count = lax.axis_size(axis)
    if count != 2:
        return lax.all_gather(value, axis, axis=0, tiled=True)
    other = lax.ppermute(value, axis, [(0, 1), (1, 0)])
    first = lax.axis_index(axis) == 0
    return jnp.concatenate([jnp.where(first, value, other), jnp.where(first, other, value)], 0)


def digits(count):
    if count % 4:
        return [(count, 1)]
    return [(size, stride) for size, stride in ((count // 4, 4), (2, 2), (2, 1)) if size > 1]


def staged_scatter(value, axis, reverse, scale):
    parts = digits(lax.axis_size(axis))
    me = lax.axis_index(axis)
    count = lax.axis_size(axis)
    rows = value.shape[0] // count
    value = value.reshape(tuple(size for size, _ in parts) + (rows,) + value.shape[1:])
    order = list(range(len(parts)))[::-1]
    if reverse:
        order = order[:1] + order[1:][::-1]
    for dim in order:
        size, stride = parts[dim]
        own = lax.rem(lax.div(me, stride), size)
        total = lax.dynamic_index_in_dim(value, own, dim)
        for step in range(1, size):
            sent = lax.dynamic_index_in_dim(value, lax.rem(own + step, size), dim)
            moves = []
            for source in range(count):
                digit = source // stride % size
                moves.append((source, source + ((digit + step) % size - digit) * stride))
            got = lax.ppermute((sent * scale).astype(jnp.float16), axis, moves)
            total = total + got.astype(jnp.float32) * (1.0 / scale)
        value = total
    return value.reshape((rows,) + value.shape[-1:])


def half_scale(rows):
    bound = 13.0 * math.sqrt(rows) * 1.05
    return 2.0 ** math.floor(math.log2(65504.0 / bound))


def orth(part):
    gram = lax.dot_general(part, part, (((0,), (0,)), ((), ())), precision=HIGHEST)
    lower = inverse_factor(whole_sum(gram))
    return lax.dot_general(part, lower, (((1,), (1,)), ((), ())), precision=HIGHEST)


def per_device(counts, row_support, col_support, total, sketch):
    row_local, col_local = gather_supports(row_support, col_support)
    table = lift(counts, row_local, col_local, total)
    total_rows = table.shape[0] * lax.axis_size("row")
    total_cols = table.shape[1] * lax.axis_size("col")

    first = sum_scatter(jnp.dot(table, sketch, preferred_element_type=jnp.float32), "col")
    q_first = gather(orth(first).astype(jnp.bfloat16), "col")
    partial_value = lax.dot_general(
        table, q_first, (((0,), (0,)), ((), ())), preferred_element_type=jnp.float32
    )
    half = partial_value.shape[1] // 2
    scale = half_scale(total_rows)
    second = jnp.concatenate(
        [
            staged_scatter(partial_value[:, :half], "row", False, scale),
            staged_scatter(partial_value[:, half:], "row", True, scale),
        ],
        1,
    )
    q_second = lax.all_gather(orth(second).astype(jnp.bfloat16), "row", axis=0, tiled=True)
    third = sum_scatter(jnp.dot(table, q_second, preferred_element_type=jnp.float32), "col")
    q_third = gather(orth(third) * jnp.sqrt(jnp.float32(total_rows)), "col")
    return q_third, q_second.astype(jnp.float32) * jnp.sqrt(jnp.float32(total_cols))


def solution(mesh):
    in_specs = (P("row", "col"), P(("row", "col")), P(("col", "row")), P(), P("col", None))
    out_specs = (P("row", None), P("col", None))
    return jax.shard_map(
        per_device, mesh=mesh, in_specs=in_specs, out_specs=out_specs, check_vma=False
    )
```

```python
import functools
import math

import jax
import jax.numpy as jnp
from jax import lax
from jax.experimental import pallas as pl
from jax.experimental.pallas import tpu as pltpu
from jax.sharding import PartitionSpec as P

HIGHEST = lax.Precision.HIGHEST
MESH = pl.DeviceIdType.MESH
BLOCK = 32


def lift(block, row_part, col_part, total):
    value = jnp.log(jnp.maximum(block, 1).astype(jnp.float32))
    value = value + jnp.log(total[0].astype(jnp.float32))
    value = value - jnp.log(row_part.astype(jnp.float32))[:, None]
    value = value - jnp.log(col_part.astype(jnp.float32))[None, :]
    return jnp.where(block > 0, jnp.maximum(value, 0.0), 0.0).astype(jnp.bfloat16)


def factor_step(rest, inverse, lower_ref, base):
    size = rest.shape[0]
    lanes = 128
    corner = rest[:BLOCK, :lanes]
    row = lax.broadcasted_iota(jnp.int32, (BLOCK, lanes), 0)
    lane = lax.broadcasted_iota(jnp.int32, (BLOCK, lanes), 1)
    unit = jnp.where(lane - BLOCK == row, 1.0, 0.0)
    work = jnp.where(lane < BLOCK, corner, unit)
    pivots = jnp.ones((BLOCK, 1), jnp.float32)
    for j in range(BLOCK):
        pivot = work[j : j + 1, j : j + 1]
        scaled = work[j : j + 1, :] * (1.0 / pivot)
        column = jnp.where(row > j, work[:, j : j + 1], 0.0)
        work = work - column * scaled
        pivots = jnp.where(row[:, :1] == j, pivot, pivots)
    work = work * lax.rsqrt(pivots)
    small = pltpu.roll(work, lanes - BLOCK, 1)[:, :BLOCK]
    panel = jnp.dot(small, rest[:BLOCK, :], precision=HIGHEST, preferred_element_type=jnp.float32)
    done = jnp.dot(small, inverse[:BLOCK, :], precision=HIGHEST, preferred_element_type=jnp.float32)
    lower_ref[pl.ds(pl.multiple_of(base, BLOCK), BLOCK), :] = done
    panel = pltpu.roll(panel, size - BLOCK, 1)
    down = (((0,), (0,)), ((), ()))
    rest_cut = lax.dot_general(panel, panel, down, precision=HIGHEST, preferred_element_type=jnp.float32)
    inverse_cut = lax.dot_general(panel, done, down, precision=HIGHEST, preferred_element_type=jnp.float32)
    return rest_cut, inverse_cut


def invert_factor(gram_ref, lower_ref, rest_ref, inverse_ref):
    size = gram_ref.shape[0]
    rest_ref[:size, :] = gram_ref[...]
    rest_ref[size:, :] = jnp.zeros((BLOCK, size), jnp.float32)
    row = lax.broadcasted_iota(jnp.int32, (size, size), 0)
    lane = lax.broadcasted_iota(jnp.int32, (size, size), 1)
    inverse_ref[:size, :] = jnp.where(row == lane, 1.0, 0.0)
    inverse_ref[size:, :] = jnp.zeros((BLOCK, size), jnp.float32)

    def body(step, carry):
        rest_cut, inverse_cut = factor_step(rest_ref[:size, :], inverse_ref[:size, :], lower_ref, step * BLOCK)
        rest_ref[:size, :] = pltpu.roll(rest_ref[BLOCK:, :], size - BLOCK, 1) - rest_cut
        inverse_ref[:size, :] = inverse_ref[BLOCK:, :] - inverse_cut
        return carry

    lax.fori_loop(0, size // BLOCK, body, 0)


def inverse_factor(gram):
    size = gram.shape[0]
    return pl.pallas_call(
        invert_factor,
        out_shape=jax.ShapeDtypeStruct((size, size), jnp.float32),
        in_specs=[pl.BlockSpec(memory_space=pltpu.VMEM)],
        out_specs=pl.BlockSpec(memory_space=pltpu.VMEM),
        scratch_shapes=[
            pltpu.VMEM((size + BLOCK, size), jnp.float32),
            pltpu.VMEM((size + BLOCK, size), jnp.float32),
        ],
    )(gram)


def place(index, cols):
    return (lax.div(index, cols), lax.rem(index, cols))


def greet(count, cols, me):
    barrier = pltpu.get_barrier_semaphore()

    def hello(step, carry):
        peer = lax.rem(me + step, count)
        pl.semaphore_signal(barrier, inc=1, device_id=place(peer, cols), device_id_type=MESH)
        return carry

    lax.fori_loop(1, count, hello, 0)
    pl.semaphore_wait(barrier, count - 1)


def reduce_kernel(count, cols, part_ref, total_ref, inbox, mine, send_a, recv_a, send_b, recv_b):
    me = lax.axis_index("row") * cols + lax.axis_index("col")
    rows = part_ref.shape[0] // count
    greet(count, cols, me)

    def rows_of(index):
        return pl.ds(pl.multiple_of(index * rows, rows), rows)

    def scatter_copy(step):
        peer = lax.rem(me + step, count)
        return pltpu.make_async_remote_copy(
            src_ref=part_ref.at[rows_of(peer), :],
            dst_ref=inbox.at[me],
            send_sem=send_a.at[step],
            recv_sem=recv_a.at[me],
            device_id=place(peer, cols),
            device_id_type=MESH,
        )

    def arrival(step):
        peer = lax.rem(me + count - step, count)
        return pltpu.make_async_remote_copy(
            src_ref=part_ref.at[rows_of(me), :],
            dst_ref=inbox.at[peer],
            send_sem=send_a.at[step],
            recv_sem=recv_a.at[peer],
            device_id=place(peer, cols),
            device_id_type=MESH,
        )

    def spread_copy(step):
        peer = lax.rem(me + step, count)
        return pltpu.make_async_remote_copy(
            src_ref=mine,
            dst_ref=total_ref.at[rows_of(me), :],
            send_sem=send_b.at[step],
            recv_sem=recv_b.at[me],
            device_id=place(peer, cols),
            device_id_type=MESH,
        )

    def spread_arrival(step):
        peer = lax.rem(me + count - step, count)
        return pltpu.make_async_remote_copy(
            src_ref=mine,
            dst_ref=total_ref.at[rows_of(peer), :],
            send_sem=send_b.at[step],
            recv_sem=recv_b.at[peer],
            device_id=place(peer, cols),
            device_id_type=MESH,
        )

    def each(action):
        def body(step, carry):
            action(step)
            return carry

        lax.fori_loop(1, count, body, 0)

    each(lambda step: scatter_copy(step).start())
    inbox[me] = part_ref[rows_of(me), :]
    each(lambda step: arrival(step).wait_recv())
    total = inbox[0]
    for index in range(1, count):
        total = total + inbox[index]
    mine[...] = total
    each(lambda step: spread_copy(step).start())
    total_ref[rows_of(me), :] = total
    each(lambda step: spread_arrival(step).wait_recv())
    each(lambda step: scatter_copy(step).wait_send())
    each(lambda step: spread_copy(step).wait_send())


def whole_sum(value):
    cols = lax.axis_size("col")
    count = lax.axis_size("row") * cols
    size, width = value.shape
    rows = size // count
    if size % (8 * count) or width % 128:
        return lax.psum(value, ("row", "col"))
    sems = pltpu.SemaphoreType.DMA((count,))
    return pl.pallas_call(
        functools.partial(reduce_kernel, count, cols),
        out_shape=jax.ShapeDtypeStruct(value.shape, value.dtype),
        in_specs=[pl.BlockSpec(memory_space=pltpu.VMEM)],
        out_specs=pl.BlockSpec(memory_space=pltpu.VMEM),
        scratch_shapes=[
            pltpu.VMEM((count, rows, width), value.dtype),
            pltpu.VMEM((rows, width), value.dtype),
            sems,
            sems,
            sems,
            sems,
        ],
        compiler_params=pltpu.CompilerParams(collective_id=0, has_side_effects=True),
    )(value)


def support_kernel(n_row, n_col, row_ref, col_ref, row_all, col_all, send_sem, recv_sem):
    row, col = lax.axis_index("row"), lax.axis_index("col")

    def across(step):
        return (row, lax.rem(col + step, n_col))

    def down(step):
        return (lax.rem(row + step, n_row), col)

    barrier = pltpu.get_barrier_semaphore()
    peers = [across(step) for step in range(1, n_col)] + [down(step) for step in range(1, n_row)]
    for peer in peers:
        pl.semaphore_signal(barrier, inc=1, device_id=peer, device_id_type=MESH)
    pl.semaphore_wait(barrier, len(peers))

    def copy(ref, into, slot, lane, peer):
        return pltpu.make_async_remote_copy(
            src_ref=ref,
            dst_ref=into.at[slot],
            send_sem=send_sem.at[lane],
            recv_sem=recv_sem.at[lane],
            device_id=peer,
            device_id_type=MESH,
        )

    sends, waits = [], []
    for step in range(1, n_col):
        lane = step - 1
        sends.append(copy(row_ref, row_all, col, lane, across(step)))
        waits.append(copy(row_ref, row_all, lax.rem(col + n_col - step, n_col), lane, across(step)))
    for step in range(1, n_row):
        lane = n_col - 1 + step - 1
        sends.append(copy(col_ref, col_all, row, lane, down(step)))
        waits.append(copy(col_ref, col_all, lax.rem(row + n_row - step, n_row), lane, down(step)))
    for item in sends:
        item.start()
    row_all[col] = row_ref[...]
    col_all[row] = col_ref[...]
    for item in waits:
        item.wait_recv()
    for item in sends:
        item.wait_send()


def gather_supports(row_support, col_support):
    n_row, n_col = lax.axis_size("row"), lax.axis_size("col")
    row_len, col_len = row_support.shape[0], col_support.shape[0]
    if row_len % 128 or col_len % 128:
        row_local = lax.all_gather(row_support, "col", axis=0, tiled=True)
        return row_local, lax.all_gather(col_support, "row", axis=0, tiled=True)
    lanes = n_row + n_col - 2
    vmem = pl.BlockSpec(memory_space=pltpu.VMEM)
    row_all, col_all = pl.pallas_call(
        functools.partial(support_kernel, n_row, n_col),
        out_shape=[
            jax.ShapeDtypeStruct((n_col, row_len // 128, 128), row_support.dtype),
            jax.ShapeDtypeStruct((n_row, col_len // 128, 128), col_support.dtype),
        ],
        in_specs=[vmem, vmem],
        out_specs=[vmem, vmem],
        scratch_shapes=[pltpu.SemaphoreType.DMA((lanes,)), pltpu.SemaphoreType.DMA((lanes,))],
        compiler_params=pltpu.CompilerParams(collective_id=1, has_side_effects=True),
    )(row_support.reshape(-1, 128), col_support.reshape(-1, 128))
    return row_all.reshape(-1), col_all.reshape(-1)


def sum_scatter(value, axis):
    count = lax.axis_size(axis)
    if count != 2:
        return lax.psum_scatter(value, axis, scatter_dimension=0, tiled=True)
    here = lax.axis_index(axis)
    rows = value.shape[0] // 2
    sent = lax.dynamic_slice_in_dim(value, (1 - here) * rows, rows, 0)
    got = lax.ppermute(sent, axis, [(0, 1), (1, 0)])
    return lax.dynamic_slice_in_dim(value, here * rows, rows, 0) + got


def gather(value, axis):
    count = lax.axis_size(axis)
    if count != 2:
        return lax.all_gather(value, axis, axis=0, tiled=True)
    other = lax.ppermute(value, axis, [(0, 1), (1, 0)])
    first = lax.axis_index(axis) == 0
    return jnp.concatenate([jnp.where(first, value, other), jnp.where(first, other, value)], 0)


def digits(count):
    if count % 4:
        return [(count, 1)]
    return [(size, stride) for size, stride in ((count // 4, 4), (2, 2), (2, 1)) if size > 1]


def staged_scatter(value, axis, reverse, scale):
    parts = digits(lax.axis_size(axis))
    me = lax.axis_index(axis)
    count = lax.axis_size(axis)
    rows = value.shape[0] // count
    value = value.reshape(tuple(size for size, _ in parts) + (rows,) + value.shape[1:])
    order = list(range(len(parts)))[::-1]
    if reverse:
        order = order[:1] + order[1:][::-1]
    for dim in order:
        size, stride = parts[dim]
        own = lax.rem(lax.div(me, stride), size)
        total = lax.dynamic_index_in_dim(value, own, dim)
        for step in range(1, size):
            sent = lax.dynamic_index_in_dim(value, lax.rem(own + step, size), dim)
            moves = []
            for source in range(count):
                digit = source // stride % size
                moves.append((source, source + ((digit + step) % size - digit) * stride))
            got = lax.ppermute((sent * scale).astype(jnp.float16), axis, moves)
            total = total + got.astype(jnp.float32) * (1.0 / scale)
        value = total
    return value.reshape((rows,) + value.shape[-1:])


def staged_gather(value, axis, reverse):
    count = lax.axis_size(axis)
    parts = digits(count)
    me = lax.axis_index(axis)
    rows, width = value.shape
    value = value.reshape((1,) * len(parts) + value.shape)
    order = list(range(len(parts)))
    if reverse:
        order = order[:-1][::-1] + order[-1:]
    for dim in order:
        size, stride = parts[dim]
        own = lax.rem(lax.div(me, stride), size)
        shape = value.shape[:dim] + (size,) + value.shape[dim + 1 :]
        whole = lax.dynamic_update_slice_in_dim(jnp.zeros(shape, value.dtype), value, own, dim)
        for step in range(1, size):
            moves = []
            for source in range(count):
                digit = source // stride % size
                moves.append((source, source + ((digit + step) % size - digit) * stride))
            got = lax.ppermute(value, axis, moves)
            whole = lax.dynamic_update_slice_in_dim(whole, got, lax.rem(own + size - step, size), dim)
        value = whole
    return value.reshape(count * rows, width)


def half_scale(rows):
    bound = 13.0 * math.sqrt(rows) * 1.05
    return 2.0 ** math.floor(math.log2(65504.0 / bound))


def orth(part):
    gram = lax.dot_general(part, part, (((0,), (0,)), ((), ())), precision=HIGHEST)
    lower = inverse_factor(whole_sum(gram))
    return lax.dot_general(part, lower, (((1,), (1,)), ((), ())), precision=HIGHEST)


def per_device(counts, row_support, col_support, total, sketch):
    row_local, col_local = gather_supports(row_support, col_support)
    table = lift(counts, row_local, col_local, total)
    total_rows = table.shape[0] * lax.axis_size("row")
    total_cols = table.shape[1] * lax.axis_size("col")

    first = sum_scatter(jnp.dot(table, sketch, preferred_element_type=jnp.float32), "col")
    q_first = gather(orth(first).astype(jnp.bfloat16), "col")
    partial_value = lax.dot_general(
        table, q_first, (((0,), (0,)), ((), ())), preferred_element_type=jnp.float32
    )
    half = partial_value.shape[1] // 2
    scale = half_scale(total_rows)
    second = jnp.concatenate(
        [
            staged_scatter(partial_value[:, :half], "row", False, scale),
            staged_scatter(partial_value[:, half:], "row", True, scale),
        ],
        1,
    )
    q_own = orth(second).astype(jnp.bfloat16)
    q_second = jnp.concatenate(
        [staged_gather(q_own[:, :half], "row", False), staged_gather(q_own[:, half:], "row", True)], 1
    )
    third = sum_scatter(jnp.dot(table, q_second, preferred_element_type=jnp.float32), "col")
    q_third = gather(orth(third) * jnp.sqrt(jnp.float32(total_rows)), "col")
    return q_third, q_second.astype(jnp.float32) * jnp.sqrt(jnp.float32(total_cols))


def solution(mesh):
    in_specs = (P("row", "col"), P(("row", "col")), P(("col", "row")), P(), P("col", None))
    out_specs = (P("row", None), P("col", None))
    return jax.shard_map(
        per_device, mesh=mesh, in_specs=in_specs, out_specs=out_specs, check_vma=False
    )
```
